512 devices in a mesh: param: 16 (over y, x), dom: 32 (over z, core).
Axes of the slice: x: 4, y: 4, z: 16, core: 2. Of those that a mesh axis runs over, the one named last changes fastest.
Arguments:
- particles: bfloat16 [512, 524288], P('dom', 'param'), may hold values from -40 to 40
- scores: bfloat16 [512, 524288], P('dom', 'param'), may hold values from -6 to 6
- basis: bfloat16 [524288, 128], P(('param', 'dom')), may hold values from -0.0078125 to 0.0078125
Outputs:
- velocity: bfloat16 [512, 524288], P('dom', 'param')
- phi: float32 [512, 128], P('dom')
The draws below stay inside these ranges and needn't reach their ends.
All inputs are finite; a program needn't handle non-finite values.
Results may differ from the reference program's by a relative error of at most 0.0049.
Values may be sent and summed in bfloat16 or wider, within the bound.
No kernel may reach another device: no remote copies, remote signals or barrier semaphores. Data moves between devices by JAX's collectives and lax.ppermute only.
A program may use at most 64 MiB of HBM per device.

```python
import math
import jax
import jax.numpy as jnp
from jax import lax

P_SIZE = 524288
R = 128
M = 512


def draw_particles(key, part):
    first, second = jax.random.split(jax.random.fold_in(key, 11), 2)
    rows = jnp.arange(M, dtype=jnp.float32)
    jitter = jax.random.uniform(second, (M,), jnp.float32, -1.1, 1.1)
    scale = jnp.power(3.0, rows / M) * jnp.exp(jitter)
    base = jax.random.normal(first, (M, P_SIZE), jnp.float32)
    return jnp.clip(base * scale[:, None], -40.0, 40.0).astype(jnp.bfloat16)


def block_levels(own_key, dims, cuts, least, largest):
    def one(position, blocks):
        draws = jax.random.uniform(jax.random.fold_in(jax.random.fold_in(own_key, 6), position), (blocks,), jnp.float32, least / len(cuts), largest / len(cuts))
        return jnp.repeat(jnp.exp(draws), dims[position] // blocks).reshape((-1,) + (1,) * (len(dims) - position - 1))

    factor_of = one(*cuts[0])
    for cut in cuts[1:]:
        factor_of = factor_of * one(*cut)
    return factor_of


def centred(key, dims, scale, reach, shards=(), kind=jnp.bfloat16):
    loudness = block_levels(key, dims, shards, -0.22, 0.18) if shards else 1.0
    array = jax.random.normal(key, dims, jnp.float32) * scale * loudness
    return jnp.minimum(jnp.maximum(array, -reach), reach).astype(kind)


def setup_inputs(seed: int = 0) -> dict:
    streams_of = jax.random.split(jax.random.key(seed), 4)
    return {
        "particles": draw_particles(jax.random.fold_in(streams_of[3], 71), 0),
        "scores": centred(streams_of[1], (M, P_SIZE), 1.0, 6.0, ((0, 32), (1, 16))),
        "basis": centred(streams_of[2], (P_SIZE, R), P_SIZE ** -0.5, 0.0078125, ((0, 512),)),
    }


def stein_terms(own, every, every_score):
    count = every.shape[0]
    every_sq = lax.optimization_barrier(jnp.sum(every * every, axis=1))
    own_sq = lax.optimization_barrier(jnp.sum(own * own, axis=1))
    center = lax.optimization_barrier(jnp.mean(every, axis=0))
    width = 2.0 * (jnp.mean(every_sq) - jnp.sum(center * center)) / math.log(count) + 1e-06
    cross = jnp.dot(own, every.T, precision=lax.Precision.HIGHEST)
    dist = own_sq[:, None] + every_sq[None, :] - 2.0 * cross
    kern = jnp.exp(-dist / width)
    drive = jnp.dot(kern, every_score, precision=lax.Precision.HIGHEST)
    pull = jnp.dot(kern, every, precision=lax.Precision.HIGHEST)
    total = lax.optimization_barrier(jnp.sum(kern, axis=1))
    return (drive + 2.0 / width * (own * total[:, None] - pull)) / count

def reference(particles, scores, basis):
    coeffs = jnp.dot(particles, basis, preferred_element_type=jnp.float32)
    score_coeffs = jnp.dot(scores, basis, preferred_element_type=jnp.float32)
    phi = stein_terms(coeffs, coeffs, score_coeffs)
    lift = math.sqrt(P_SIZE / R)
    lifted = jnp.dot(phi.astype(jnp.bfloat16), basis.T, preferred_element_type=jnp.float32)
    velocity = (lifted * lift).astype(jnp.bfloat16)
    return (velocity, phi)
```

```python
import math

import jax
import jax.numpy as jnp
from jax import lax
from jax.sharding import Mesh, PartitionSpec as P

P_SIZE = 524288
R = 128
TAIL = 16
TOP = 15.0


def swap_cores(array):
    return lax.ppermute(array, "core", [(0, 1), (1, 0)])


def packed_shard(basis):
    wide = basis.astype(jnp.float32)
    largest = jnp.maximum(jnp.max(jnp.abs(wide)), 1e-30)
    power = jnp.ceil(jnp.log2(largest))
    scaled = (wide * jnp.exp2(TOP - power)).astype(jnp.float16)
    tail = jnp.full((TAIL, basis.shape[1]), power, jnp.float32).astype(jnp.float16)
    return jnp.concatenate([scaled, tail], axis=0)


def unpacked(gathered, shards):
    rows = gathered.reshape(shards, -1, gathered.shape[1])
    power = rows[:, -TAIL:, :].astype(jnp.float32)[:, :1, :1]
    wide = rows[:, :-TAIL, :].astype(jnp.float32) * jnp.exp2(power - TOP)
    return wide.astype(jnp.bfloat16)


def stein_terms(own, every, every_score):
    count = every.shape[0]
    every_sq = jnp.sum(every * every, axis=1)
    own_sq = jnp.sum(own * own, axis=1)
    center = jnp.mean(every, axis=0)
    width = 2.0 * (jnp.mean(every_sq) - jnp.sum(center * center)) / math.log(count) + 1e-06
    cross = jnp.dot(own, every.T, precision=lax.Precision.HIGHEST)
    dist = own_sq[:, None] + every_sq[None, :] - 2.0 * cross
    kern = jnp.exp(-dist / width)
    drive = jnp.dot(kern, every_score, precision=lax.Precision.HIGHEST)
    pull = jnp.dot(kern, every, precision=lax.Precision.HIGHEST)
    total = jnp.sum(kern, axis=1)
    return (drive + 2.0 / width * (own * total[:, None] - pull)) / count


def sent_to_all(array, axis):
    peers = lax.axis_size(axis)
    return lax.all_to_all(
        jnp.broadcast_to(array[None], (peers, *array.shape)), axis, 0, 0, tiled=True
    )


def contract(rows, half_basis):
    return lax.dot_general(
        rows, half_basis, (((1, 2), (0, 1)), ((), ())), preferred_element_type=jnp.float32
    )


def lift(phi_low, half_basis):
    lifted = lax.dot_general(
        phi_low, half_basis, (((1,), (2,)), ((), ())), preferred_element_type=jnp.float32
    )
    return (lifted * math.sqrt(P_SIZE / R)).astype(jnp.bfloat16)


def body(particles, scores, basis):
    rows = particles.shape[0]
    depth = basis.shape[0]
    shards = lax.axis_size("z")
    core = lax.axis_index("core")
    both = jnp.concatenate([particles, scores], axis=0).reshape(2 * rows, shards, 2, depth)
    theirs = lax.dynamic_index_in_dim(both, 1 - core, 2, keepdims=False)
    mine = lax.dynamic_index_in_dim(both, core, 2, keepdims=False)
    others = swap_cores(theirs)
    gathered = lax.all_gather(packed_shard(basis), "z", axis=0, tiled=True)
    half = unpacked(gathered, shards)
    other_half = swap_cores(half)
    own_part = contract(mine, half)
    other_part = contract(others, half)
    own_part = jnp.concatenate([own_part[:rows], own_part[rows:]], axis=1)
    other_part = jnp.concatenate([other_part[:rows], other_part[rows:]], axis=1)
    first = jnp.where(core == 0, own_part, other_part)
    second = jnp.where(core == 0, other_part, own_part)
    pair = jnp.stack([first, second])
    peers = lax.axis_size("param")
    pieces = jnp.broadcast_to(pair[None], (peers, *pair.shape)).reshape(2 * peers, rows, -1)
    summed = lax.all_to_all(pieces, ("param", "core"), 0, 0, tiled=True).sum(axis=0)
    column = sent_to_all(summed, "z").reshape(shards * rows, -1)
    everyone = lax.all_gather(column, "core", axis=0, tiled=True)
    phi = stein_terms(summed[:, :R], everyone[:, :R], everyone[:, R:])
    phi_low = phi.astype(jnp.bfloat16)
    ours = lift(phi_low, half)
    rest = lift(phi_low, other_half)
    low = jnp.where(core == 0, ours, rest)
    high = jnp.where(core == 0, rest, ours)
    velocity = jnp.stack([low, high], axis=2).reshape(particles.shape)
    return (velocity, phi)


def solution(mesh):
    inner = Mesh(mesh.devices.reshape(mesh.devices.shape[0], -1, 2), ("param", "z", "core"))
    dom = ("z", "core")
    in_specs = (P(dom, "param"), P(dom, "param"), P(("param", "z", "core"), None))
    out_specs = (P(dom, "param"), P(dom, None))
    return jax.shard_map(body, mesh=inner, in_specs=in_specs, out_specs=out_specs, check_vma=False)
```

```python
import math

import jax
import jax.numpy as jnp
from jax import lax
from jax.experimental import pallas as pl
from jax.experimental.pallas import tpu as pltpu
from jax.sharding import Mesh, PartitionSpec as P

P_SIZE = 524288
R = 128
TAIL = 16
TOP = 15.0
HIGHEST = lax.Precision.HIGHEST
ACROSS = (((1,), (1,)), ((), ()))
CHUNKS = 4
VMEM = pl.BlockSpec(memory_space=pltpu.VMEM)
ANY = pl.BlockSpec(memory_space=pl.ANY)
SMEM = pl.BlockSpec(memory_space=pltpu.SMEM)


def swap_cores(array):
    return lax.ppermute(array, "core", [(0, 1), (1, 0)])


def packed_shard(basis):
    wide = basis.astype(jnp.float32)
    largest = jnp.maximum(jnp.max(jnp.abs(wide)), 1e-30)
    power = jnp.ceil(jnp.log2(largest))
    scaled = (wide * jnp.exp2(TOP - power)).astype(jnp.float16)
    tail = jnp.full((TAIL, basis.shape[1]), power, jnp.float32).astype(jnp.float16)
    return jnp.concatenate([scaled, tail], axis=0)


def unpacked(gathered, shards):
    rows = gathered.reshape(shards, -1, gathered.shape[1])
    power = rows[:, -TAIL:, :].astype(jnp.float32)[:, :1, :1]
    wide = rows[:, :-TAIL, :].astype(jnp.float32) * jnp.exp2(power - TOP)
    return wide.astype(jnp.bfloat16)


def chunk_copies(source_ref, target_ref, sems):
    size = source_ref.shape[0] // CHUNKS
    return [
        pltpu.make_async_copy(
            source_ref.at[pl.ds(k * size, size)], target_ref.at[pl.ds(k * size, size)], sems.at[k]
        )
        for k in range(CHUNKS)
    ]


def contract_kernel(core_ref, p_ref, s_ref, other_p_ref, other_s_ref, half_hbm, out_ref, half_ref, sems):
    core = core_ref[0]
    shards, depth, cols = half_ref.shape
    rows = p_ref.shape[0]
    copies = chunk_copies(half_hbm, half_ref, sems)
    for copy in copies:
        copy.start()
    total = jnp.zeros((4 * rows, cols), jnp.float32)
    for i in range(shards):
        if i % (shards // CHUNKS) == 0:
            copies[i // (shards // CHUNKS)].wait()
        at = pl.ds(pl.multiple_of((2 * i + core) * depth, depth), depth)
        block = jnp.concatenate([r[:, at] for r in (p_ref, s_ref, other_p_ref, other_s_ref)], axis=0)
        total += jnp.dot(block, half_ref[i], preferred_element_type=jnp.float32)
    own = jnp.concatenate([total[:rows], total[rows : 2 * rows]], axis=1)
    other = jnp.concatenate([total[2 * rows : 3 * rows], total[3 * rows :]], axis=1)
    out_ref[core] = own
    out_ref[1 - core] = other


def contract(core, particles, scores, other_p, other_s, half):
    rows, cols = particles.shape[0], half.shape[2]
    return pl.pallas_call(
        contract_kernel,
        out_shape=jax.ShapeDtypeStruct((2, rows, 2 * cols), jnp.float32),
        in_specs=[SMEM] + [VMEM] * 4 + [ANY],
        out_specs=VMEM,
        scratch_shapes=[pltpu.VMEM(half.shape, half.dtype), pltpu.SemaphoreType.DMA((CHUNKS,))],
        compiler_params=pltpu.CompilerParams(vmem_limit_bytes=24 << 20),
        cost_estimate=pl.CostEstimate(
            flops=2 * 4 * rows * half.size, bytes_accessed=2 * half.size, transcendentals=0
        ),
    )(core, particles, scores, other_p, other_s, half)


def stein_terms(own, both):
    count, cols = both.shape[0], own.shape[1]
    every = both[:, :cols]
    squares = every * every
    center = jnp.sum(every, axis=0, keepdims=True) / count
    mean_sq = jnp.sum(squares) / count
    width = 2.0 * (mean_sq - jnp.sum(center * center)) / math.log(count) + 1e-06
    every_sq = lax.dot_general(
        jnp.ones_like(own), squares, ACROSS, precision=HIGHEST, preferred_element_type=jnp.float32
    )
    cross = lax.dot_general(
        own, every, ACROSS, precision=HIGHEST, preferred_element_type=jnp.float32
    )
    dist = jnp.sum(own * own, axis=1, keepdims=True) + every_sq - 2.0 * cross
    kern = jnp.exp(-dist / width)
    pulled = jnp.dot(kern, both, precision=HIGHEST, preferred_element_type=jnp.float32)
    total = jnp.sum(kern, axis=1, keepdims=True)
    return (pulled[:, cols:] + (2.0 / width) * (own * total - pulled[:, :cols])) / count


def finish_kernel(
    core_ref, own_ref, every_ref, half_hbm, other_hbm, velocity_hbm, phi_ref,
    half_ref, other_ref, velocity_ref, half_sems, other_sems, out_sems,
):
    core = core_ref[0]
    shards, depth, cols = half_ref.shape
    copies = tuple(
        zip(
            chunk_copies(half_hbm, half_ref, half_sems),
            chunk_copies(other_hbm, other_ref, other_sems),
        )
    )
    for pair in copies:
        for copy in pair:
            copy.start()
    phi = stein_terms(own_ref[:, :cols], every_ref[...])
    phi_ref[...] = phi
    low = phi.astype(jnp.bfloat16)
    scale = math.sqrt(P_SIZE / R)
    each = shards // CHUNKS
    span = 2 * each * depth
    outs = []
    for k in range(CHUNKS):
        for copy in copies[k]:
            copy.wait()
        for i in range(k * each, (k + 1) * each):
            for ref, place in ((half_ref, core), (other_ref, 1 - core)):
                lifted = lax.dot_general(low, ref[i], ACROSS, preferred_element_type=jnp.float32)
                at = pl.ds(pl.multiple_of((2 * i + place) * depth, depth), depth)
                velocity_ref[:, at] = (lifted * scale).astype(jnp.bfloat16)
        part = pl.ds(k * span, span)
        out = pltpu.make_async_copy(velocity_ref.at[:, part], velocity_hbm.at[:, part], out_sems.at[k])
        out.start()
        outs.append(out)
    for out in outs:
        out.wait()


def finish(core, own, everyone, half, other_half):
    rows, cols = own.shape[0], half.shape[2]
    dims = 2 * half.shape[0] * half.shape[1]
    sems = pltpu.SemaphoreType.DMA((CHUNKS,))
    return pl.pallas_call(
        finish_kernel,
        out_shape=(
            jax.ShapeDtypeStruct((rows, dims), jnp.bfloat16),
            jax.ShapeDtypeStruct((rows, cols), jnp.float32),
        ),
        in_specs=[SMEM, VMEM, VMEM, ANY, ANY],
        out_specs=(ANY, VMEM),
        scratch_shapes=[
            pltpu.VMEM(half.shape, half.dtype),
            pltpu.VMEM(half.shape, half.dtype),
            pltpu.VMEM((rows, dims), jnp.bfloat16),
            sems,
            sems,
            sems,
        ],
        compiler_params=pltpu.CompilerParams(vmem_limit_bytes=24 << 20),
        cost_estimate=pl.CostEstimate(
            flops=4 * rows * half.size, bytes_accessed=4 * half.size, transcendentals=0
        ),
    )(core, own, everyone, half, other_half)


def sent_to_all(array, axis):
    peers = lax.axis_size(axis)
    return lax.all_to_all(
        jnp.broadcast_to(array[None], (peers, *array.shape)), axis, 0, 0, tiled=True
    )


def body(particles, scores, basis):
    rows = particles.shape[0]
    shards = lax.axis_size("z")
    peers = lax.axis_size("param")
    core = lax.axis_index("core").astype(jnp.int32)[None]
    other_p = swap_cores(particles)
    other_s = swap_cores(scores)
    packed, other_p, other_s = lax.optimization_barrier((packed_shard(basis), other_p, other_s))
    gathered = lax.all_gather(packed, "z", axis=0, tiled=True)
    half = unpacked(gathered, shards)
    other_half = swap_cores(half)
    pair = contract(core, particles, scores, other_p, other_s, half)
    pieces = jnp.broadcast_to(pair[None], (peers, *pair.shape)).reshape(2 * peers, rows, -1)
    summed = lax.all_to_all(pieces, ("param", "core"), 0, 0, tiled=True).sum(axis=0)
    column = sent_to_all(summed, "z").reshape(shards * rows, -1)
    everyone = lax.all_gather(column, "core", axis=0, tiled=True)
    velocity, phi = finish(core, summed, everyone, half, other_half)
    return (velocity, phi)


def solution(mesh):
    inner = Mesh(mesh.devices.reshape(mesh.devices.shape[0], -1, 2), ("param", "z", "core"))
    dom = ("z", "core")
    in_specs = (P(dom, "param"), P(dom, "param"), P(("param", "z", "core"), None))
    out_specs = (P(dom, "param"), P(dom, None))
    return jax.shard_map(body, mesh=inner, in_specs=in_specs, out_specs=out_specs, check_vma=False)
```

```python
import math

import jax
import jax.numpy as jnp
from jax import lax
from jax.experimental import pallas as pl
from jax.experimental.pallas import tpu as pltpu
from jax.sharding import Mesh, PartitionSpec as P

P_SIZE = 524288
R = 128
TAIL = 16
TOP = 15.0
HIGHEST = lax.Precision.HIGHEST
ACROSS = (((1,), (1,)), ((), ()))
CHUNKS = 4
PIECES = 8
VMEM = pl.BlockSpec(memory_space=pltpu.VMEM)
HBM = pl.BlockSpec(memory_space=pltpu.HBM)
SMEM = pl.BlockSpec(memory_space=pltpu.SMEM)


def swap_cores(array):
    return lax.ppermute(array, "core", [(0, 1), (1, 0)])


def prepare_kernel(
    core_ref, p_hbm, s_hbm, basis_hbm, theirs_ref, packed_ref, basis_ref, sems, basis_sem
):
    core = core_ref[0]
    rows = p_hbm.shape[0]
    depth = basis_ref.shape[0]
    fetch = pltpu.make_async_copy(basis_hbm, basis_ref, basis_sem)
    fetch.start()
    copies = []
    for k, source in enumerate((p_hbm, s_hbm)):
        for i in range(theirs_ref.shape[1] // depth):
            at = pl.ds(pl.multiple_of((2 * i + 1 - core) * depth, depth), depth)
            target = theirs_ref.at[pl.ds(k * rows, rows), pl.ds(i * depth, depth)]
            copies.append(pltpu.make_async_copy(source.at[:, at], target, sems.at[k, i]))
    for copy in copies:
        copy.start()
    fetch.wait()
    wide = basis_ref[...].astype(jnp.float32)
    largest = jnp.max(jnp.max(jnp.abs(wide), axis=0, keepdims=True), axis=1, keepdims=True)
    power = jnp.ceil(jnp.log2(jnp.maximum(largest, 1e-30)))
    packed_ref[:depth] = (wide * jnp.exp2(TOP - power)).astype(jnp.bfloat16)
    packed_ref[depth:] = jnp.broadcast_to(power, (TAIL, wide.shape[1])).astype(jnp.bfloat16)
    for copy in copies:
        copy.wait()


def prepare(core, particles, scores, basis):
    rows, cols = particles.shape
    depth = basis.shape[0]
    return pl.pallas_call(
        prepare_kernel,
        out_shape=(
            jax.ShapeDtypeStruct((2 * rows, cols // 2), particles.dtype),
            jax.ShapeDtypeStruct((depth + TAIL, basis.shape[1]), jnp.bfloat16),
        ),
        in_specs=[SMEM, HBM, HBM, HBM],
        out_specs=(VMEM, VMEM),
        scratch_shapes=[
            pltpu.VMEM(basis.shape, basis.dtype),
            pltpu.SemaphoreType.DMA((2, cols // 2 // depth)),
            pltpu.SemaphoreType.DMA,
        ],
        cost_estimate=pl.CostEstimate(
            flops=2 * basis.size, bytes_accessed=4 * particles.size, transcendentals=0
        ),
    )(core, particles, scores, basis)


def unpacked(gathered, shards):
    rows = gathered.reshape(shards, -1, gathered.shape[1])
    power = rows[:, -TAIL:, :].astype(jnp.float32)[:, :1, :1]
    wide = rows[:, :-TAIL, :].astype(jnp.float32) * jnp.exp2(power - TOP)
    return wide.astype(jnp.bfloat16)


def chunk_copies(source_ref, target_ref, sems):
    chunks = sems.shape[0]
    size = source_ref.shape[0] // chunks
    return [
        pltpu.make_async_copy(
            source_ref.at[pl.ds(k * size, size)], target_ref.at[pl.ds(k * size, size)], sems.at[k]
        )
        for k in range(chunks)
    ]


def contract_kernel(core_ref, p_ref, s_ref, others_ref, half_hbm, out_ref, half_ref, sems):
    core = core_ref[0]
    shards, depth, cols = half_ref.shape
    rows = p_ref.shape[0]
    copies = chunk_copies(half_hbm, half_ref, sems)
    for copy in copies:
        copy.start()
    total = jnp.zeros((4 * rows, cols), jnp.float32)
    for i in range(shards):
        if i % (shards // CHUNKS) == 0:
            copies[i // (shards // CHUNKS)].wait()
        at = pl.ds(pl.multiple_of((2 * i + core) * depth, depth), depth)
        theirs = others_ref[:, i * depth : (i + 1) * depth]
        block = jnp.concatenate([p_ref[:, at], s_ref[:, at], theirs], axis=0)
        total += jnp.dot(block, half_ref[i], preferred_element_type=jnp.float32)
    own = jnp.concatenate([total[:rows], total[rows : 2 * rows]], axis=1)
    other = jnp.concatenate([total[2 * rows : 3 * rows], total[3 * rows :]], axis=1)
    out_ref[core] = own
    out_ref[1 - core] = other


def contract(core, particles, scores, others, half):
    rows, cols = particles.shape[0], half.shape[2]
    return pl.pallas_call(
        contract_kernel,
        out_shape=jax.ShapeDtypeStruct((2, rows, 2 * cols), jnp.float32),
        in_specs=[SMEM] + [VMEM] * 3 + [HBM],
        out_specs=VMEM,
        scratch_shapes=[pltpu.VMEM(half.shape, half.dtype), pltpu.SemaphoreType.DMA((CHUNKS,))],
        compiler_params=pltpu.CompilerParams(vmem_limit_bytes=24 << 20),
        cost_estimate=pl.CostEstimate(
            flops=2 * 4 * rows * half.size, bytes_accessed=2 * half.size, transcendentals=0
        ),
    )(core, particles, scores, others, half)


def stein_terms(own, both):
    count, cols = both.shape[0], own.shape[1]
    every = both[:, :cols]
    squares = jnp.sum(every * every, axis=1, keepdims=True)
    center = jnp.sum(every, axis=0, keepdims=True) / count
    mean_sq = jnp.sum(squares) / count
    width = 2.0 * (mean_sq - jnp.sum(center * center)) / math.log(count) + 1e-06
    every_sq = jnp.broadcast_to(squares, (count, cols)).T[: own.shape[0]]
    cross = lax.dot_general(
        own, every, ACROSS, precision=HIGHEST, preferred_element_type=jnp.float32
    )
    dist = jnp.sum(own * own, axis=1, keepdims=True) + every_sq - 2.0 * cross
    kern = jnp.exp(-dist / width)
    pulled = jnp.dot(kern, both, precision=HIGHEST, preferred_element_type=jnp.float32)
    total = jnp.sum(kern, axis=1, keepdims=True)
    return (pulled[:, cols:] + (2.0 / width) * (own * total - pulled[:, :cols])) / count


def finish_kernel(
    core_ref, own_ref, every_ref, half_hbm, other_hbm, velocity_hbm, phi_ref,
    half_ref, other_ref, velocity_ref, half_sems, other_sems, out_sems,
):
    core = core_ref[0]
    shards, depth, cols = half_ref.shape
    copies = tuple(
        zip(
            chunk_copies(half_hbm, half_ref, half_sems),
            chunk_copies(other_hbm, other_ref, other_sems),
        )
    )
    for pair in copies:
        for copy in pair:
            copy.start()
    phi = stein_terms(own_ref[:, :cols], every_ref[...])
    phi_ref[...] = phi
    low = phi.astype(jnp.bfloat16)
    scale = math.sqrt(P_SIZE / R)
    each = shards // PIECES
    span = 2 * each * depth
    outs = []
    for k in range(PIECES):
        for copy in copies[k]:
            copy.wait()
        for i in range(k * each, (k + 1) * each):
            for ref, place in ((half_ref, core), (other_ref, 1 - core)):
                lifted = lax.dot_general(low, ref[i], ACROSS, preferred_element_type=jnp.float32)
                at = pl.ds(pl.multiple_of((2 * i + place) * depth, depth), depth)
                velocity_ref[:, at] = (lifted * scale).astype(jnp.bfloat16)
        part = pl.ds(k * span, span)
        out = pltpu.make_async_copy(velocity_ref.at[:, part], velocity_hbm.at[:, part], out_sems.at[k])
        out.start()
        outs.append(out)
    for out in outs:
        out.wait()


def finish(core, own, everyone, half, other_half):
    rows, cols = own.shape[0], half.shape[2]
    dims = 2 * half.shape[0] * half.shape[1]
    sems = pltpu.SemaphoreType.DMA((PIECES,))
    return pl.pallas_call(
        finish_kernel,
        out_shape=(
            jax.ShapeDtypeStruct((rows, dims), jnp.bfloat16),
            jax.ShapeDtypeStruct((rows, cols), jnp.float32),
        ),
        in_specs=[SMEM, VMEM, VMEM, HBM, HBM],
        out_specs=(HBM, VMEM),
        scratch_shapes=[
            pltpu.VMEM(half.shape, half.dtype),
            pltpu.VMEM(half.shape, half.dtype),
            pltpu.VMEM((rows, dims), jnp.bfloat16),
            sems,
            sems,
            sems,
        ],
        compiler_params=pltpu.CompilerParams(vmem_limit_bytes=24 << 20),
        cost_estimate=pl.CostEstimate(
            flops=4 * rows * half.size, bytes_accessed=4 * half.size, transcendentals=0
        ),
    )(core, own, everyone, half, other_half)


def sent_to_all(array, axis):
    peers = lax.axis_size(axis)
    return lax.all_to_all(
        jnp.broadcast_to(array[None], (peers, *array.shape)), axis, 0, 0, tiled=True
    )


def body(particles, scores, basis):
    rows = particles.shape[0]
    shards = lax.axis_size("z")
    peers = lax.axis_size("param")
    core = lax.axis_index("core").astype(jnp.int32)[None]
    theirs, packed = prepare(core, particles, scores, basis)
    others = swap_cores(theirs)
    gathered = lax.all_gather(packed.astype(jnp.float16), "z", axis=0, tiled=True)
    half = unpacked(gathered, shards)
    pair = contract(core, particles, scores, others, half)
    pair, held = lax.optimization_barrier((pair, half))
    other_half = swap_cores(held)
    pieces = jnp.broadcast_to(pair[None], (peers, *pair.shape)).reshape(2 * peers, rows, -1)
    summed = lax.all_to_all(pieces, ("param", "core"), 0, 0, tiled=True).sum(axis=0)
    column = sent_to_all(summed, "z").reshape(shards * rows, -1)
    everyone = lax.all_gather(column, "core", axis=0, tiled=True)
    velocity, phi = finish(core, summed, everyone, half, other_half)
    return (velocity, phi)


def solution(mesh):
    inner = Mesh(mesh.devices.reshape(mesh.devices.shape[0], -1, 2), ("param", "z", "core"))
    dom = ("z", "core")
    in_specs = (P(dom, "param"), P(dom, "param"), P(("param", "z", "core"), None))
    out_specs = (P(dom, "param"), P(dom, None))
    return jax.shard_map(body, mesh=inner, in_specs=in_specs, out_specs=out_specs, check_vma=False)
```

```python
import math

import jax
import jax.numpy as jnp
from jax import lax
from jax.experimental import pallas as pl
from jax.experimental.pallas import tpu as pltpu
from jax.sharding import Mesh, PartitionSpec as P

P_SIZE = 524288
R = 128
TAIL = 16
TOP = 15.0
HIGHEST = lax.Precision.HIGHEST
ACROSS = (((1,), (1,)), ((), ()))
CHUNKS = 4
PIECES = 8
VMEM = pl.BlockSpec(memory_space=pltpu.VMEM)
HBM = pl.BlockSpec(memory_space=pltpu.HBM)
SMEM = pl.BlockSpec(memory_space=pltpu.SMEM)


def swap_cores(array):
    return lax.ppermute(array, "core", [(0, 1), (1, 0)])


def prepare_kernel(
    core_ref, p_hbm, s_hbm, basis_hbm, theirs_ref, packed_ref, basis_ref, sems, basis_sem
):
    core = core_ref[0]
    rows = p_hbm.shape[0]
    depth = basis_ref.shape[0]
    fetch = pltpu.make_async_copy(basis_hbm, basis_ref, basis_sem)
    fetch.start()
    copies = []
    for k, source in enumerate((p_hbm, s_hbm)):
        for i in range(theirs_ref.shape[1] // depth):
            at = pl.ds(pl.multiple_of((2 * i + 1 - core) * depth, depth), depth)
            target = theirs_ref.at[pl.ds(k * rows, rows), pl.ds(i * depth, depth)]
            copies.append(pltpu.make_async_copy(source.at[:, at], target, sems.at[k, i]))
    for copy in copies:
        copy.start()
    fetch.wait()
    wide = basis_ref[...].astype(jnp.float32)
    largest = jnp.max(jnp.max(jnp.abs(wide), axis=0, keepdims=True), axis=1, keepdims=True)
    power = jnp.ceil(jnp.log2(jnp.maximum(largest, 1e-30)))
    packed_ref[:depth] = (wide * jnp.exp2(TOP - power)).astype(jnp.bfloat16)
    packed_ref[depth:] = jnp.broadcast_to(power, (TAIL, wide.shape[1])).astype(jnp.bfloat16)
    for copy in copies:
        copy.wait()


def prepare(core, particles, scores, basis):
    rows, cols = particles.shape
    depth = basis.shape[0]
    return pl.pallas_call(
        prepare_kernel,
        out_shape=(
            jax.ShapeDtypeStruct((2 * rows, cols // 2), particles.dtype),
            jax.ShapeDtypeStruct((depth + TAIL, basis.shape[1]), jnp.bfloat16),
        ),
        in_specs=[SMEM, HBM, HBM, HBM],
        out_specs=(VMEM, VMEM),
        scratch_shapes=[
            pltpu.VMEM(basis.shape, basis.dtype),
            pltpu.SemaphoreType.DMA((2, cols // 2 // depth)),
            pltpu.SemaphoreType.DMA,
        ],
        cost_estimate=pl.CostEstimate(
            flops=2 * basis.size, bytes_accessed=4 * particles.size, transcendentals=0
        ),
    )(core, particles, scores, basis)


def unpacked(gathered, shards):
    rows = gathered.reshape(shards, -1, gathered.shape[1])
    power = rows[:, -TAIL:, :].astype(jnp.float32)[:, :1, :1]
    wide = rows[:, :-TAIL, :].astype(jnp.float32) * jnp.exp2(power - TOP)
    return wide.astype(jnp.bfloat16)


def chunk_copies(source_ref, target_ref, sems):
    chunks = sems.shape[0]
    size = source_ref.shape[0] // chunks
    return [
        pltpu.make_async_copy(
            source_ref.at[pl.ds(k * size, size)], target_ref.at[pl.ds(k * size, size)], sems.at[k]
        )
        for k in range(chunks)
    ]


def contract_kernel(core_ref, p_ref, s_ref, others_ref, half_ref, out_ref, kept_hbm, sems):
    core = core_ref[0]
    shards, depth, cols = half_ref.shape
    rows = p_ref.shape[0]
    copies = chunk_copies(half_ref, kept_hbm, sems)
    for copy in copies:
        copy.start()
    total = jnp.zeros((4 * rows, cols), jnp.float32)
    for i in range(shards):
        at = pl.ds(pl.multiple_of((2 * i + core) * depth, depth), depth)
        theirs = others_ref[:, i * depth : (i + 1) * depth]
        block = jnp.concatenate([p_ref[:, at], s_ref[:, at], theirs], axis=0)
        total += jnp.dot(block, half_ref[i], preferred_element_type=jnp.float32)
    own = jnp.concatenate([total[:rows], total[rows : 2 * rows]], axis=1)
    other = jnp.concatenate([total[2 * rows : 3 * rows], total[3 * rows :]], axis=1)
    out_ref[core] = own
    out_ref[1 - core] = other
    for copy in copies:
        copy.wait()


def contract(core, particles, scores, others, half):
    rows, cols = particles.shape[0], half.shape[2]
    return pl.pallas_call(
        contract_kernel,
        out_shape=(
            jax.ShapeDtypeStruct((2, rows, 2 * cols), jnp.float32),
            jax.ShapeDtypeStruct(half.shape, half.dtype),
        ),
        in_specs=[SMEM] + [VMEM] * 4,
        out_specs=(VMEM, HBM),
        scratch_shapes=[pltpu.SemaphoreType.DMA((CHUNKS,))],
        compiler_params=pltpu.CompilerParams(vmem_limit_bytes=24 << 20),
        cost_estimate=pl.CostEstimate(
            flops=2 * 4 * rows * half.size, bytes_accessed=2 * half.size, transcendentals=0
        ),
    )(core, particles, scores, others, half)


def stein_terms(own, both):
    count, cols = both.shape[0], own.shape[1]
    every = both[:, :cols]
    squares = jnp.sum(every * every, axis=1, keepdims=True)
    center = jnp.sum(every, axis=0, keepdims=True) / count
    mean_sq = jnp.sum(squares) / count
    width = 2.0 * (mean_sq - jnp.sum(center * center)) / math.log(count) + 1e-06
    every_sq = jnp.broadcast_to(squares, (count, cols)).T[: own.shape[0]]
    cross = lax.dot_general(
        own, every, ACROSS, precision=HIGHEST, preferred_element_type=jnp.float32
    )
    dist = jnp.sum(own * own, axis=1, keepdims=True) + every_sq - 2.0 * cross
    kern = jnp.exp(-dist / width)
    pulled = jnp.dot(kern, both, precision=HIGHEST, preferred_element_type=jnp.float32)
    total = jnp.sum(kern, axis=1, keepdims=True)
    return (pulled[:, cols:] + (2.0 / width) * (own * total - pulled[:, :cols])) / count


def finish_kernel(
    core_ref, own_ref, every_ref, half_hbm, other_hbm, velocity_hbm, phi_ref,
    half_ref, other_ref, velocity_ref, half_sems, other_sems, out_sems,
):
    core = core_ref[0]
    shards, depth, cols = half_ref.shape
    copies = tuple(
        zip(
            chunk_copies(half_hbm, half_ref, half_sems),
            chunk_copies(other_hbm, other_ref, other_sems),
        )
    )
    for pair in copies:
        for copy in pair:
            copy.start()
    phi = stein_terms(own_ref[:, :cols], every_ref[...])
    phi_ref[...] = phi
    low = phi.astype(jnp.bfloat16)
    scale = math.sqrt(P_SIZE / R)
    each = shards // PIECES
    span = 2 * each * depth
    outs = []
    for k in range(PIECES):
        for copy in copies[k]:
            copy.wait()
        for i in range(k * each, (k + 1) * each):
            for ref, place in ((half_ref, core), (other_ref, 1 - core)):
                lifted = lax.dot_general(low, ref[i], ACROSS, preferred_element_type=jnp.float32)
                at = pl.ds(pl.multiple_of((2 * i + place) * depth, depth), depth)
                velocity_ref[:, at] = (lifted * scale).astype(jnp.bfloat16)
        part = pl.ds(k * span, span)
        out = pltpu.make_async_copy(velocity_ref.at[:, part], velocity_hbm.at[:, part], out_sems.at[k])
        out.start()
        outs.append(out)
    for out in outs:
        out.wait()


def finish(core, own, everyone, half, other_half):
    rows, cols = own.shape[0], half.shape[2]
    dims = 2 * half.shape[0] * half.shape[1]
    sems = pltpu.SemaphoreType.DMA((PIECES,))
    return pl.pallas_call(
        finish_kernel,
        out_shape=(
            jax.ShapeDtypeStruct((rows, dims), jnp.bfloat16),
            jax.ShapeDtypeStruct((rows, cols), jnp.float32),
        ),
        in_specs=[SMEM, VMEM, VMEM, HBM, HBM],
        out_specs=(HBM, VMEM),
        scratch_shapes=[
            pltpu.VMEM(half.shape, half.dtype),
            pltpu.VMEM(half.shape, half.dtype),
            pltpu.VMEM((rows, dims), jnp.bfloat16),
            sems,
            sems,
            sems,
        ],
        compiler_params=pltpu.CompilerParams(vmem_limit_bytes=24 << 20),
        cost_estimate=pl.CostEstimate(
            flops=4 * rows * half.size, bytes_accessed=4 * half.size, transcendentals=0
        ),
    )(core, own, everyone, half, other_half)


def sent_to_all(array, axis):
    peers = lax.axis_size(axis)
    return lax.all_to_all(
        jnp.broadcast_to(array[None], (peers, *array.shape)), axis, 0, 0, tiled=True
    )


def body(particles, scores, basis):
    rows = particles.shape[0]
    shards = lax.axis_size("z")
    peers = lax.axis_size("param")
    core = lax.axis_index("core").astype(jnp.int32)[None]
    theirs, packed = prepare(core, particles, scores, basis)
    others = swap_cores(theirs)
    gathered = lax.all_gather(packed.astype(jnp.float16), "z", axis=0, tiled=True)
    pair, half = contract(core, particles, scores, others, unpacked(gathered, shards))
    other_half = swap_cores(half)
    pieces = jnp.broadcast_to(pair[None], (peers, *pair.shape)).reshape(2 * peers, rows, -1)
    summed = lax.all_to_all(pieces, ("param", "core"), 0, 0, tiled=True).sum(axis=0)
    column = sent_to_all(summed, "z").reshape(shards * rows, -1)
    everyone = lax.all_gather(column, "core", axis=0, tiled=True)
    velocity, phi = finish(core, summed, everyone, half, other_half)
    return (velocity, phi)


def solution(mesh):
    inner = Mesh(mesh.devices.reshape(mesh.devices.shape[0], -1, 2), ("param", "z", "core"))
    dom = ("z", "core")
    in_specs = (P(dom, "param"), P(dom, "param"), P(("param", "z", "core"), None))
    out_specs = (P(dom, "param"), P(dom, None))
    return jax.shard_map(body, mesh=inner, in_specs=in_specs, out_specs=out_specs, check_vma=False)
```

```python
import math

import jax
import jax.numpy as jnp
from jax import lax
from jax.experimental import pallas as pl
from jax.experimental.pallas import tpu as pltpu
from jax.sharding import Mesh, PartitionSpec as P

P_SIZE = 524288
R = 128
TAIL = 16
TOP = 15.0
HIGHEST = lax.Precision.HIGHEST
ACROSS = (((1,), (1,)), ((), ()))
CHUNKS = 4
PIECES = 8
VMEM = pl.BlockSpec(memory_space=pltpu.VMEM)
HBM = pl.BlockSpec(memory_space=pltpu.HBM)
SMEM = pl.BlockSpec(memory_space=pltpu.SMEM)


def swap_cores(array):
    return lax.ppermute(array, "core", [(0, 1), (1, 0)])


def prepare_kernel(
    core_ref, p_hbm, s_hbm, basis_hbm, theirs_hbm, packed_ref,
    basis_ref, theirs_ref, sems, basis_sem, out_sems,
):
    core = core_ref[0]
    rows = p_hbm.shape[0]
    depth = basis_ref.shape[0]
    fetch = pltpu.make_async_copy(basis_hbm, basis_ref, basis_sem)
    fetch.start()
    copies = []
    for k, source in enumerate((p_hbm, s_hbm)):
        for i in range(theirs_ref.shape[1] // depth):
            at = pl.ds(pl.multiple_of((2 * i + 1 - core) * depth, depth), depth)
            target = theirs_ref.at[pl.ds(k * rows, rows), pl.ds(i * depth, depth)]
            copies.append(pltpu.make_async_copy(source.at[:, at], target, sems.at[k, i]))
    for copy in copies:
        copy.start()
    outs = []
    for k in range(2):
        for copy in copies[k * len(copies) // 2 : (k + 1) * len(copies) // 2]:
            copy.wait()
        part = pl.ds(k * rows, rows)
        out = pltpu.make_async_copy(theirs_ref.at[part], theirs_hbm.at[part], out_sems.at[k])
        out.start()
        outs.append(out)
    fetch.wait()
    wide = basis_ref[...].astype(jnp.float32)
    largest = jnp.max(jnp.max(jnp.abs(wide), axis=0, keepdims=True), axis=1, keepdims=True)
    power = jnp.ceil(jnp.log2(jnp.maximum(largest, 1e-30)))
    packed_ref[:depth] = (wide * jnp.exp2(TOP - power)).astype(jnp.bfloat16)
    packed_ref[depth:] = jnp.broadcast_to(power, (TAIL, wide.shape[1])).astype(jnp.bfloat16)
    for out in outs:
        out.wait()


def prepare(core, particles, scores, basis):
    rows, cols = particles.shape
    depth = basis.shape[0]
    return pl.pallas_call(
        prepare_kernel,
        out_shape=(
            jax.ShapeDtypeStruct((2 * rows, cols // 2), particles.dtype),
            jax.ShapeDtypeStruct((depth + TAIL, basis.shape[1]), jnp.bfloat16),
        ),
        in_specs=[SMEM, HBM, HBM, HBM],
        out_specs=(HBM, VMEM),
        scratch_shapes=[
            pltpu.VMEM(basis.shape, basis.dtype),
            pltpu.VMEM((2 * rows, cols // 2), particles.dtype),
            pltpu.SemaphoreType.DMA((2, cols // 2 // depth)),
            pltpu.SemaphoreType.DMA,
            pltpu.SemaphoreType.DMA((2,)),
        ],
        cost_estimate=pl.CostEstimate(
            flops=2 * basis.size, bytes_accessed=4 * particles.size, transcendentals=0
        ),
    )(core, particles, scores, basis)


def unpacked(gathered, shards):
    rows = gathered.reshape(shards, -1, gathered.shape[1])
    power = rows[:, -TAIL:, :].astype(jnp.float32)[:, :1, :1]
    wide = rows[:, :-TAIL, :].astype(jnp.float32) * jnp.exp2(power - TOP)
    return wide.astype(jnp.bfloat16)


def chunk_copies(source_ref, target_ref, sems):
    chunks = sems.shape[0]
    size = source_ref.shape[0] // chunks
    return [
        pltpu.make_async_copy(
            source_ref.at[pl.ds(k * size, size)], target_ref.at[pl.ds(k * size, size)], sems.at[k]
        )
        for k in range(chunks)
    ]


def contract_kernel(core_ref, p_ref, s_ref, others_ref, half_ref, out_ref, kept_hbm, sems):
    core = core_ref[0]
    shards, depth, cols = half_ref.shape
    rows = p_ref.shape[0]
    copies = chunk_copies(half_ref, kept_hbm, sems)
    for copy in copies:
        copy.start()
    total = jnp.zeros((4 * rows, cols), jnp.float32)
    for i in range(shards):
        at = pl.ds(pl.multiple_of((2 * i + core) * depth, depth), depth)
        theirs = others_ref[:, i * depth : (i + 1) * depth]
        block = jnp.concatenate([p_ref[:, at], s_ref[:, at], theirs], axis=0)
        total += jnp.dot(block, half_ref[i], preferred_element_type=jnp.float32)
    own = jnp.concatenate([total[:rows], total[rows : 2 * rows]], axis=1)
    other = jnp.concatenate([total[2 * rows : 3 * rows], total[3 * rows :]], axis=1)
    out_ref[core] = own
    out_ref[1 - core] = other
    for copy in copies:
        copy.wait()


def contract(core, particles, scores, others, half):
    rows, cols = particles.shape[0], half.shape[2]
    return pl.pallas_call(
        contract_kernel,
        out_shape=(
            jax.ShapeDtypeStruct((2, rows, 2 * cols), jnp.float32),
            jax.ShapeDtypeStruct(half.shape, half.dtype),
        ),
        in_specs=[SMEM] + [VMEM] * 4,
        out_specs=(VMEM, HBM),
        scratch_shapes=[pltpu.SemaphoreType.DMA((CHUNKS,))],
        compiler_params=pltpu.CompilerParams(vmem_limit_bytes=24 << 20),
        cost_estimate=pl.CostEstimate(
            flops=2 * 4 * rows * half.size, bytes_accessed=2 * half.size, transcendentals=0
        ),
    )(core, particles, scores, others, half)


def stein_terms(own, both):
    count, cols = both.shape[0], own.shape[1]
    every = both[:, :cols]
    squares = jnp.sum(every * every, axis=1, keepdims=True)
    center = jnp.sum(every, axis=0, keepdims=True) / count
    mean_sq = jnp.sum(squares) / count
    width = 2.0 * (mean_sq - jnp.sum(center * center)) / math.log(count) + 1e-06
    every_sq = jnp.broadcast_to(squares, (count, cols)).T[: own.shape[0]]
    cross = lax.dot_general(
        own, every, ACROSS, precision=HIGHEST, preferred_element_type=jnp.float32
    )
    dist = jnp.sum(own * own, axis=1, keepdims=True) + every_sq - 2.0 * cross
    kern = jnp.exp(-dist / width)
    pulled = jnp.dot(kern, both, precision=HIGHEST, preferred_element_type=jnp.float32)
    total = jnp.sum(kern, axis=1, keepdims=True)
    return (pulled[:, cols:] + (2.0 / width) * (own * total - pulled[:, :cols])) / count


def finish_kernel(
    core_ref, own_ref, every_ref, half_hbm, other_hbm, velocity_hbm, phi_hbm,
    half_ref, other_ref, velocity_ref, phi_ref, half_sems, other_sems, out_sems, phi_sem,
):
    core = core_ref[0]
    shards, depth, cols = half_ref.shape
    copies = tuple(
        zip(
            chunk_copies(half_hbm, half_ref, half_sems),
            chunk_copies(other_hbm, other_ref, other_sems),
        )
    )
    for pair in copies:
        for copy in pair:
            copy.start()
    phi = stein_terms(own_ref[:, :cols], every_ref[...])
    phi_ref[...] = phi
    phi_out = pltpu.make_async_copy(phi_ref, phi_hbm, phi_sem)
    phi_out.start()
    low = phi.astype(jnp.bfloat16)
    scale = math.sqrt(P_SIZE / R)
    each = shards // PIECES
    span = 2 * each * depth
    outs = [phi_out]
    for k in range(PIECES):
        for copy in copies[k]:
            copy.wait()
        for i in range(k * each, (k + 1) * each):
            for ref, place in ((half_ref, core), (other_ref, 1 - core)):
                lifted = lax.dot_general(low, ref[i], ACROSS, preferred_element_type=jnp.float32)
                at = pl.ds(pl.multiple_of((2 * i + place) * depth, depth), depth)
                velocity_ref[:, at] = (lifted * scale).astype(jnp.bfloat16)
        part = pl.ds(k * span, span)
        out = pltpu.make_async_copy(velocity_ref.at[:, part], velocity_hbm.at[:, part], out_sems.at[k])
        out.start()
        outs.append(out)
    for out in outs:
        out.wait()


def finish(core, own, everyone, half, other_half):
    rows, cols = own.shape[0], half.shape[2]
    dims = 2 * half.shape[0] * half.shape[1]
    sems = pltpu.SemaphoreType.DMA((PIECES,))
    return pl.pallas_call(
        finish_kernel,
        out_shape=(
            jax.ShapeDtypeStruct((rows, dims), jnp.bfloat16),
            jax.ShapeDtypeStruct((rows, cols), jnp.float32),
        ),
        in_specs=[SMEM, VMEM, VMEM, HBM, HBM],
        out_specs=(HBM, HBM),
        scratch_shapes=[
            pltpu.VMEM(half.shape, half.dtype),
            pltpu.VMEM(half.shape, half.dtype),
            pltpu.VMEM((rows, dims), jnp.bfloat16),
            pltpu.VMEM((rows, cols), jnp.float32),
            sems,
            sems,
            sems,
            pltpu.SemaphoreType.DMA,
        ],
        compiler_params=pltpu.CompilerParams(vmem_limit_bytes=24 << 20),
        cost_estimate=pl.CostEstimate(
            flops=4 * rows * half.size, bytes_accessed=4 * half.size, transcendentals=0
        ),
    )(core, own, everyone, half, other_half)


def sent_to_all(array, axis):
    peers = lax.axis_size(axis)
    return lax.all_to_all(
        jnp.broadcast_to(array[None], (peers, *array.shape)), axis, 0, 0, tiled=True
    )


def body(particles, scores, basis):
    rows = particles.shape[0]
    shards = lax.axis_size("z")
    peers = lax.axis_size("param")
    core = lax.axis_index("core").astype(jnp.int32)[None]
    theirs, packed = prepare(core, particles, scores, basis)
    others = swap_cores(theirs)
    gathered = lax.all_gather(packed.astype(jnp.float16), "z", axis=0, tiled=True)
    pair, half = contract(core, particles, scores, others, unpacked(gathered, shards))
    other_half = swap_cores(half)
    pieces = jnp.broadcast_to(pair[None], (peers, *pair.shape)).reshape(2 * peers, rows, -1)
    summed = lax.all_to_all(pieces, ("param", "core"), 0, 0, tiled=True).sum(axis=0)
    column = sent_to_all(summed, "z").reshape(shards * rows, -1)
    everyone = lax.all_gather(column, "core", axis=0, tiled=True)
    velocity, phi = finish(core, summed, everyone, half, other_half)
    return (velocity, phi)


def solution(mesh):
    inner = Mesh(mesh.devices.reshape(mesh.devices.shape[0], -1, 2), ("param", "z", "core"))
    dom = ("z", "core")
    in_specs = (P(dom, "param"), P(dom, "param"), P(("param", "z", "core"), None))
    out_specs = (P(dom, "param"), P(dom, None))
    return jax.shard_map(body, mesh=inner, in_specs=in_specs, out_specs=out_specs, check_vma=False)
```
